32 devices in a mesh: tm: 4 (over y, x), space: 8 (over z, core).
Axes of the slice: x: 2, y: 2, z: 4, core: 2. Of those that a mesh axis runs over, the one named last changes fastest.
Arguments:
- signal: bfloat16 [16, 256, 512], P('space', None, 'tm'), may hold values from -6 to 6
- source_boxes: int32 [16, 12], replicated, may hold values from 0 to 15
- near_boxes: int32 [16, 8], replicated, may hold values from 0 to 15, as said below
- trans_kernel: float32 [12, 256, 128], P(None, 'space'), may hold values from -0.15625 to 0.15625
- near_kernel: float32 [8, 128], replicated, may hold values from -0.1875 to 0.1875
Outputs:
- field: bfloat16 [16, 256, 512], P('space', None, 'tm')
The draws below stay inside these ranges and needn't reach their ends.
Inputs may be any that keep to these rules, and one draw needn't show every extreme that they name: Each near_boxes[b, j] lies within 2 of b.
All inputs are finite; a program needn't handle non-finite values.
Results may differ from the reference program's by a relative error of at most 0.008.
Values may be sent and summed in bfloat16 or wider, within the bound.
A program may use at most 192 MiB of HBM per device.

```python
import jax
import jax.numpy as jnp
from jax import lax

R = 256
OFFSETS = 12
NEAR = 8
REACH = 2
TB = 128
BOXES = 16
SAMPLES = 512
N_TM = 4


def draw_near_boxes(key, part):
    boxes = jnp.arange(BOXES, dtype=jnp.int32)[:, None]
    moves = jax.random.randint(jax.random.fold_in(key, 17), (BOXES, NEAR), -REACH, REACH + 1, dtype=jnp.int32)
    return jnp.clip(boxes + moves, 0, BOXES - 1).astype(jnp.int32)


def plant(entries, rng, smallest, largest):
    longest = entries.shape.index(max(entries.shape))
    spots = []
    for shift in (0, 1):
        where = [jax.random.randint(jax.random.fold_in(rng, axis), (), 0, length) for axis, length in enumerate(entries.shape)]
        where[longest] = (where[longest] + shift) % entries.shape[longest]
        spots.append(tuple(where))
    return entries.at[spots[0]].set(smallest).at[spots[1]].set(largest)


def level_of(rng, shape, split, low, high):
    gain, own = 1.0, jax.random.fold_in(rng, 6)
    for position, blocks in split:
        draws = jnp.exp(jax.random.uniform(jax.random.fold_in(own, position), (blocks,), jnp.float32, low / len(split), high / len(split)))
        gain = gain * jnp.repeat(draws, shape[position] // blocks).reshape([-1 if axis == position else 1 for axis in range(len(shape))])
    return gain


def normal_values(stream_key, shape, spread, most, cuts=(), kind=jnp.bfloat16):
    loudness = level_of(stream_key, shape, cuts, -0.22, 0.18) if cuts else 1.0
    entries = jax.random.normal(stream_key, shape, jnp.float32) * spread * loudness
    return jnp.minimum(jnp.maximum(entries, -most), most).astype(kind)


def setup_inputs(seed: int = 0) -> dict:
    arg_keys = jax.random.split(jax.random.key(seed), 6)
    return {
        "signal": normal_values(arg_keys[0], (BOXES, R, SAMPLES), 1.0, 6.0, ((0, 8), (2, 4))),
        "source_boxes": plant(jax.random.randint(arg_keys[1], (BOXES, OFFSETS), 0, BOXES), jax.random.fold_in(arg_keys[1], 1), 0, BOXES - 1).astype(jnp.int32),
        "near_boxes": draw_near_boxes(jax.random.fold_in(arg_keys[5], 71), 0),
        "trans_kernel": normal_values(arg_keys[3], (OFFSETS, R, TB), (OFFSETS * TB) ** -0.5, 0.15625, ((1, 8),), jnp.float32),
        "near_kernel": normal_values(arg_keys[4], (NEAR, TB), (NEAR * TB) ** -0.5, 0.1875, (), jnp.float32),
    }


def block_matrix(kernel):
    width = kernel.shape[-1]
    rows = jnp.arange(2 * width, dtype=jnp.int32)[:, None]
    cols = jnp.arange(width, dtype=jnp.int32)[None, :]
    lagged = cols + width - rows
    valid = (lagged >= 0) & (lagged < width)
    clipped = jnp.clip(lagged, 0, width - 1)
    table = jnp.take(kernel, clipped, axis=-1)
    return jnp.where(valid, table, jnp.zeros_like(table)).astype(jnp.bfloat16)


def reference(signal, source_boxes, near_boxes, trans_kernel, near_kernel):
    blocks = signal.reshape(BOXES, R, N_TM, TB)
    earlier = jnp.concatenate([jnp.zeros_like(blocks[:, :, :1]), blocks[:, :, :-1]], axis=2)
    pair = jnp.concatenate([earlier, blocks], axis=-1)
    pair = jnp.transpose(pair, (1, 0, 2, 3))
    kernels = jnp.transpose(trans_kernel, (1, 0, 2))
    near_mats = block_matrix(near_kernel).astype(jnp.float32)

    def one_ray(inputs):
        rows, kernel = inputs
        trans_mats = block_matrix(kernel).astype(jnp.float32)
        rows32 = rows.astype(jnp.float32)
        far_rows = jnp.take(rows32, source_boxes, axis=0)
        far = jnp.einsum("bkms,kst->bmt", far_rows, trans_mats)
        near_rows = jnp.take(rows32, near_boxes, axis=0)
        near = jnp.einsum("bkms,kst->bmt", near_rows, near_mats)
        return far.astype(jnp.bfloat16), near.astype(jnp.bfloat16)

    far, near = lax.map(one_ray, (pair, kernels))
    field = (far.astype(jnp.float32) + near.astype(jnp.float32)).astype(jnp.bfloat16)
    field = jnp.transpose(field, (1, 0, 2, 3))
    return field.reshape(BOXES, R, SAMPLES)
```

```python
import functools

import jax
import jax.numpy as jnp
from jax import lax
from jax.experimental import pallas as pl
from jax.experimental.pallas import tpu as pltpu
from jax.sharding import PartitionSpec as P

REACH = 2
MESH = pl.DeviceIdType.MESH
LANES = 128
SUBLANES = 8
def from_behind(shard, axis, by):
    size = lax.axis_size(axis)
    pairs = [(i, i + by) for i in range(size) if 0 <= i + by < size]
    return lax.ppermute(shard, axis, pairs)


def with_halo(block, sides, width):
    for axis, dim in sides:
        count = lax.axis_size(axis)
        forward = [(i, i + 1) for i in range(count - 1)]
        backward = [(target, source) for source, target in forward]
        low = lax.ppermute(
            lax.slice_in_dim(block, block.shape[dim] - width, None, axis=dim), axis, forward
        )
        high = lax.ppermute(lax.slice_in_dim(block, 0, width, axis=dim), axis, backward)
        block = jnp.concatenate([low, block, high], axis=dim)
    return block


def block_matrix(kernel):
    blocklen = kernel.shape[-1]
    leading = kernel.shape[:-1]
    zeroes = jnp.zeros(leading + (2 * blocklen,), jnp.bfloat16)
    widened = jnp.concatenate([zeroes, kernel.astype(jnp.bfloat16)], axis=-1)
    tiled = jnp.tile(widened, (1,) * len(leading) + (2 * blocklen,))
    trimmed = tiled[..., : 2 * blocklen * (3 * blocklen - 1)]
    skewed = trimmed.reshape(leading + (2 * blocklen, 3 * blocklen - 1))
    return skewed[..., :blocklen]


def body(signal, source_boxes, near_boxes, trans_kernel, near_kernel):
    box_dev = signal.shape[0]
    current_rays = lax.all_to_all(signal, "space", split_axis=1, concat_axis=0, tiled=True)
    earlier_rays = from_behind(current_rays, "tm", 1)
    pair_rays = jnp.concatenate([earlier_rays, current_rays], axis=-1)
    offsets = source_boxes.shape[1]
    far = jnp.zeros(current_rays.shape, jnp.float32)
    for offset in range(offsets):
        trans_mats = block_matrix(trans_kernel[offset])
        rows = jnp.take(pair_rays, source_boxes[:, offset], axis=0)
        far = far + jnp.einsum("brs,rst->brt", rows, trans_mats, preferred_element_type=jnp.float32)
    far_rays = far.astype(jnp.bfloat16)
    near_mats = block_matrix(near_kernel)
    slots = near_boxes.shape[1]
    earlier_box = from_behind(signal, "tm", 1)
    pair_box = jnp.concatenate([earlier_box, signal], axis=-1)
    padded = with_halo(pair_box, (("space", 0),), REACH)
    first = lax.axis_index("space") * box_dev
    own_near = lax.dynamic_slice_in_dim(near_boxes, first, box_dev, 0)
    local_rows = own_near - (first - REACH)
    near_sum = jnp.zeros(signal.shape, jnp.float32)
    for slot in range(slots):
        rows = jnp.take(padded, local_rows[:, slot], axis=0)
        near_sum = near_sum + jnp.einsum(
            "brs,st->brt", rows, near_mats[slot], preferred_element_type=jnp.float32
        )
    near_box = near_sum.astype(jnp.bfloat16)
    far_box = lax.all_to_all(far_rays, "space", split_axis=0, concat_axis=1, tiled=True)
    return (far_box.astype(jnp.float32) + near_box.astype(jnp.float32)).astype(jnp.bfloat16)


def fused_kernel(
    n_tm,
    n_space,
    signal_ref,
    source_ref,
    near_ref,
    trans_ref,
    kernel_ref,
    out_ref,
    landed,
    wide,
    trans_mats,
    near_mats,
    pick_far,
    pick_near,
    total,
    leaving,
    in_send,
    in_recv,
    out_send,
    out_recv,
    own_sem,
):
    peers = n_tm * n_space
    tm, space = lax.axis_index("tm"), lax.axis_index("space")
    me = tm * n_space + space
    box_dev = signal_ref.shape[0]
    boxes = n_space * box_dev
    offsets = trans_ref.shape[0]
    slots = kernel_ref.shape[0]
    rows = n_tm * boxes

    def place(linear):
        other_tm = linear // n_space
        other_space = lax.rem(linear, n_space)
        return other_tm, other_space, other_space * n_tm + other_tm

    def outbound(step):
        to_tm, to_space, group = place(lax.rem(me + step, peers))
        return pltpu.make_async_remote_copy(
            src_ref=signal_ref.at[:, group],
            dst_ref=landed.at[tm + 1, pl.ds(space * box_dev, box_dev)],
            send_sem=in_send.at[step],
            recv_sem=in_recv.at[step],
            device_id=(to_tm, to_space),
            device_id_type=MESH,
        )

    def inbound(step):
        from_tm, from_space, group = place(lax.rem(me + peers - step, peers))
        return pltpu.make_async_remote_copy(
            src_ref=signal_ref.at[:, group],
            dst_ref=landed.at[from_tm + 1, pl.ds(from_space * box_dev, box_dev)],
            send_sem=in_send.at[step],
            recv_sem=in_recv.at[step],
            device_id=(from_tm, from_space),
            device_id_type=MESH,
        )

    def homeward(step):
        to_tm, to_space, _ = place(lax.rem(me + step, peers))
        return pltpu.make_async_remote_copy(
            src_ref=leaving.at[to_tm, pl.ds(to_space * box_dev, box_dev)],
            dst_ref=out_ref.at[:, space * n_tm + tm],
            send_sem=out_send.at[step],
            recv_sem=out_recv.at[step],
            device_id=(to_tm, to_space),
            device_id_type=MESH,
        )

    def returned(step):
        from_tm, from_space, group = place(lax.rem(me + peers - step, peers))
        return pltpu.make_async_remote_copy(
            src_ref=leaving.at[from_tm, pl.ds(from_space * box_dev, box_dev)],
            dst_ref=out_ref.at[:, group],
            send_sem=out_send.at[step],
            recv_sem=out_recv.at[step],
            device_id=(from_tm, from_space),
            device_id_type=MESH,
        )

    def over_peers(action):
        def one(step, carry):
            action(step)
            return carry

        lax.fori_loop(1, peers, one, 0)

    barrier = pltpu.get_barrier_semaphore()

    def greet(step):
        to_tm, to_space, _ = place(lax.rem(me + step, peers))
        pl.semaphore_signal(barrier, inc=1, device_id=(to_tm, to_space), device_id_type=MESH)

    over_peers(greet)
    own_in = pltpu.make_async_copy(
        signal_ref.at[:, space * n_tm + tm],
        landed.at[tm + 1, pl.ds(space * box_dev, box_dev)],
        own_sem.at[0],
    )
    own_in.start()
    pl.semaphore_wait(barrier, peers - 1)
    over_peers(lambda step: outbound(step).start())

    lag = lax.broadcasted_iota(jnp.int32, (LANES, LANES), 1) - lax.broadcasted_iota(
        jnp.int32, (LANES, LANES), 0
    )
    causal = lag >= 0

    def block_rows(response):
        spread = jnp.broadcast_to(response, (LANES, LANES))
        turned = pltpu.roll(spread, 0, 1, stride=1, stride_axis=0)
        now = jnp.where(causal, turned, 0.0).astype(jnp.bfloat16)
        before = jnp.where(causal, 0.0, turned).astype(jnp.bfloat16)
        return before, now

    first_ray = pl.multiple_of(tm * SUBLANES, SUBLANES)

    def build(offset, carry):
        responses = trans_ref[offset, pl.ds(first_ray, SUBLANES), :]
        column = pl.ds(pl.multiple_of(offset * LANES, LANES), LANES)
        for ray in range(SUBLANES):
            before, now = block_rows(responses[ray : ray + 1, :])
            trans_mats[ray, 0:LANES, column] = before
            trans_mats[ray, LANES : 2 * LANES, column] = now
        return carry

    lax.fori_loop(0, offsets, build, 0)
    for slot in range(slots):
        before, now = block_rows(kernel_ref[slot : slot + 1, :])
        near_mats[0:LANES, slot * LANES : (slot + 1) * LANES] = before
        near_mats[LANES : 2 * LANES, slot * LANES : (slot + 1) * LANES] = now

    def picks(table_ref, pick_ref):
        count = table_ref.shape[1]
        row_block = lax.broadcasted_iota(jnp.int32, (rows, rows), 0) // boxes
        cols = lax.broadcasted_iota(jnp.int32, (rows, rows), 1)
        same = row_block == cols // boxes
        source = lax.rem(cols, boxes)
        for entry in range(count):
            wanted = jnp.concatenate([table_ref[:, entry : entry + 1]] * n_tm, axis=0)
            hit = jnp.logical_and(same, source == jnp.broadcast_to(wanted, (rows, rows)))
            pick_ref[:, entry * rows : (entry + 1) * rows] = jnp.where(hit, 1.0, 0.0).astype(
                jnp.bfloat16
            )

    picks(source_ref, pick_far)
    picks(near_ref, pick_near)
    landed[0] = jnp.zeros(landed.shape[1:], landed.dtype)

    own_in.wait()
    over_peers(lambda step: inbound(step).wait_recv())

    for block in range(n_tm + 1):
        wide[pl.ds(block * boxes * SUBLANES, boxes * SUBLANES), :] = (
            landed[block].astype(jnp.float32).reshape(boxes * SUBLANES, LANES)
        )

    def stacked(products, count):
        narrow = products.astype(jnp.bfloat16)
        return jnp.concatenate(
            [narrow[:, entry * LANES : (entry + 1) * LANES] for entry in range(count)], axis=0
        )

    for ray in range(SUBLANES):
        blocks = wide[pl.ds(ray, rows + boxes, stride=SUBLANES), :].astype(jnp.bfloat16)
        pair = jnp.concatenate([blocks[:rows], blocks[boxes:]], axis=1)
        far_all = jnp.dot(pair, trans_mats[ray], preferred_element_type=jnp.float32)
        far = jnp.dot(
            pick_far[...], stacked(far_all, offsets), preferred_element_type=jnp.float32
        )
        near_all = jnp.dot(pair, near_mats[...], preferred_element_type=jnp.float32)
        near = jnp.dot(
            pick_near[...], stacked(near_all, slots), preferred_element_type=jnp.float32
        )
        total[pl.ds(ray, rows, stride=SUBLANES), :] = far.astype(jnp.bfloat16).astype(
            jnp.float32
        ) + near.astype(jnp.bfloat16).astype(jnp.float32)

    for block in range(n_tm):
        leaving[block] = (
            total[pl.ds(block * boxes * SUBLANES, boxes * SUBLANES), :]
            .reshape(boxes, SUBLANES, LANES)
            .astype(jnp.bfloat16)
        )

    over_peers(lambda step: homeward(step).start())
    own_out = pltpu.make_async_copy(
        leaving.at[tm, pl.ds(space * box_dev, box_dev)],
        out_ref.at[:, space * n_tm + tm],
        own_sem.at[1],
    )
    own_out.start()
    over_peers(lambda step: outbound(step).wait_send())
    own_out.wait()
    over_peers(lambda step: returned(step).wait_recv())
    over_peers(lambda step: homeward(step).wait_send())


def fused_body(signal, source_boxes, near_boxes, trans_kernel, near_kernel):
    n_tm, n_space = lax.axis_size("tm"), lax.axis_size("space")
    peers = n_tm * n_space
    box_dev, rays, samples = signal.shape
    boxes = box_dev * n_space
    offsets, slots = trans_kernel.shape[0], near_kernel.shape[0]
    rows = n_tm * boxes
    grouped = signal.reshape(box_dev, peers, SUBLANES, samples)
    vmem = pl.BlockSpec(memory_space=pltpu.VMEM)
    anywhere = pl.BlockSpec(memory_space=pl.ANY)
    field = pl.pallas_call(
        functools.partial(fused_kernel, n_tm, n_space),
        out_shape=jax.ShapeDtypeStruct(grouped.shape, jnp.bfloat16),
        in_specs=[anywhere, vmem, vmem, vmem, vmem],
        out_specs=anywhere,
        scratch_shapes=[
            pltpu.VMEM((n_tm + 1, boxes, SUBLANES, LANES), jnp.bfloat16),
            pltpu.VMEM(((rows + boxes) * SUBLANES, LANES), jnp.float32),
            pltpu.VMEM((SUBLANES, 2 * LANES, offsets * LANES), jnp.bfloat16),
            pltpu.VMEM((2 * LANES, slots * LANES), jnp.bfloat16),
            pltpu.VMEM((rows, offsets * rows), jnp.bfloat16),
            pltpu.VMEM((rows, slots * rows), jnp.bfloat16),
            pltpu.VMEM((rows * SUBLANES, LANES), jnp.float32),
            pltpu.VMEM((n_tm, boxes, SUBLANES, LANES), jnp.bfloat16),
            pltpu.SemaphoreType.DMA((peers,)),
            pltpu.SemaphoreType.DMA((peers,)),
            pltpu.SemaphoreType.DMA((peers,)),
            pltpu.SemaphoreType.DMA((peers,)),
            pltpu.SemaphoreType.DMA((2,)),
        ],
        compiler_params=pltpu.CompilerParams(
            collective_id=0, has_side_effects=True, vmem_limit_bytes=48 * 1024 * 1024
        ),
    )(grouped, source_boxes, near_boxes, trans_kernel, near_kernel)
    return field.reshape(signal.shape)


def routed(signal, source_boxes, near_boxes, trans_kernel, near_kernel):
    n_tm, n_space = lax.axis_size("tm"), lax.axis_size("space")
    box_dev, rays, samples = signal.shape
    rows = n_tm * n_space * box_dev
    fits = rays == n_tm * n_space * SUBLANES and samples == LANES and rows <= 2 * LANES
    chosen = fused_body if fits else body
    return chosen(signal, source_boxes, near_boxes, trans_kernel, near_kernel)


def solution(mesh):
    in_specs = (P("space", None, "tm"), P(), P(), P(None, "space", None), P())
    out_specs = P("space", None, "tm")
    return jax.shard_map(
        routed, mesh=mesh, in_specs=in_specs, out_specs=out_specs, check_vma=False
    )
```

```python
import functools

import jax
import jax.numpy as jnp
from jax import lax
from jax.experimental import pallas as pl
from jax.experimental.pallas import tpu as pltpu
from jax.sharding import PartitionSpec as P

REACH = 2
MESH = pl.DeviceIdType.MESH
LANES = 128
SUBLANES = 8
def from_behind(shard, axis, by):
    size = lax.axis_size(axis)
    pairs = [(i, i + by) for i in range(size) if 0 <= i + by < size]
    return lax.ppermute(shard, axis, pairs)


def with_halo(block, sides, width):
    for axis, dim in sides:
        count = lax.axis_size(axis)
        forward = [(i, i + 1) for i in range(count - 1)]
        backward = [(target, source) for source, target in forward]
        low = lax.ppermute(
            lax.slice_in_dim(block, block.shape[dim] - width, None, axis=dim), axis, forward
        )
        high = lax.ppermute(lax.slice_in_dim(block, 0, width, axis=dim), axis, backward)
        block = jnp.concatenate([low, block, high], axis=dim)
    return block


def block_matrix(kernel):
    blocklen = kernel.shape[-1]
    leading = kernel.shape[:-1]
    zeroes = jnp.zeros(leading + (2 * blocklen,), jnp.bfloat16)
    widened = jnp.concatenate([zeroes, kernel.astype(jnp.bfloat16)], axis=-1)
    tiled = jnp.tile(widened, (1,) * len(leading) + (2 * blocklen,))
    trimmed = tiled[..., : 2 * blocklen * (3 * blocklen - 1)]
    skewed = trimmed.reshape(leading + (2 * blocklen, 3 * blocklen - 1))
    return skewed[..., :blocklen]


def body(signal, source_boxes, near_boxes, trans_kernel, near_kernel):
    box_dev = signal.shape[0]
    current_rays = lax.all_to_all(signal, "space", split_axis=1, concat_axis=0, tiled=True)
    earlier_rays = from_behind(current_rays, "tm", 1)
    pair_rays = jnp.concatenate([earlier_rays, current_rays], axis=-1)
    offsets = source_boxes.shape[1]
    far = jnp.zeros(current_rays.shape, jnp.float32)
    for offset in range(offsets):
        trans_mats = block_matrix(trans_kernel[offset])
        rows = jnp.take(pair_rays, source_boxes[:, offset], axis=0)
        far = far + jnp.einsum("brs,rst->brt", rows, trans_mats, preferred_element_type=jnp.float32)
    far_rays = far.astype(jnp.bfloat16)
    near_mats = block_matrix(near_kernel)
    slots = near_boxes.shape[1]
    earlier_box = from_behind(signal, "tm", 1)
    pair_box = jnp.concatenate([earlier_box, signal], axis=-1)
    padded = with_halo(pair_box, (("space", 0),), REACH)
    first = lax.axis_index("space") * box_dev
    own_near = lax.dynamic_slice_in_dim(near_boxes, first, box_dev, 0)
    local_rows = own_near - (first - REACH)
    near_sum = jnp.zeros(signal.shape, jnp.float32)
    for slot in range(slots):
        rows = jnp.take(padded, local_rows[:, slot], axis=0)
        near_sum = near_sum + jnp.einsum(
            "brs,st->brt", rows, near_mats[slot], preferred_element_type=jnp.float32
        )
    near_box = near_sum.astype(jnp.bfloat16)
    far_box = lax.all_to_all(far_rays, "space", split_axis=0, concat_axis=1, tiled=True)
    return (far_box.astype(jnp.float32) + near_box.astype(jnp.float32)).astype(jnp.bfloat16)


def fused_kernel(
    n_tm,
    n_space,
    signal_ref,
    source_ref,
    near_ref,
    trans_ref,
    kernel_ref,
    out_ref,
    staged,
    landed,
    wide,
    trans_rows,
    near_rows,
    trans_mats,
    near_mats,
    far_all,
    near_all,
    leaving,
    sources,
    nears,
    in_send,
    in_recv,
    out_send,
    out_recv,
    local_sem,
    stage_sem,
):
    tm, space = lax.axis_index("tm"), lax.axis_index("space")
    peers = n_tm * n_space
    box_dev = signal_ref.shape[0]
    boxes = n_space * box_dev
    offsets = trans_ref.shape[0]
    slots = kernel_ref.shape[0]
    rows = n_tm * boxes
    block_rows = boxes * SUBLANES

    def wrapped(value, size):
        return jnp.where(value >= size, value - size, value)

    others = [
        (wrapped(tm + dt, n_tm), wrapped(space + ds, n_space))
        for ds in range(n_space)
        for dt in range(n_tm)
        if dt or ds
    ]
    mine = space * n_tm + tm
    own_boxes = pl.ds(space * box_dev, box_dev)

    barrier = pltpu.get_barrier_semaphore()
    for other in others:
        pl.semaphore_signal(barrier, inc=1, device_id=other, device_id_type=MESH)
    first_ray = pl.multiple_of(tm * SUBLANES, SUBLANES)
    fetches = [
        pltpu.make_async_copy(
            trans_ref.at[:, pl.ds(first_ray, SUBLANES), :], trans_rows, local_sem.at[0]
        ),
        pltpu.make_async_copy(kernel_ref, near_rows, local_sem.at[1]),
        pltpu.make_async_copy(source_ref, sources, local_sem.at[2]),
        pltpu.make_async_copy(near_ref, nears, local_sem.at[3]),
    ]
    stagings = [
        pltpu.make_async_copy(signal_ref.at[nth], staged.at[:, nth], stage_sem.at[nth])
        for nth in range(box_dev)
    ]
    for fetch in stagings + fetches:
        fetch.start()
    pltpu.make_async_copy(signal_ref.at[:, mine], landed.at[tm + 1, own_boxes], in_recv).start()
    for staging in stagings:
        staging.wait()
    pl.semaphore_wait(barrier, peers - 1)
    for other in others:
        pltpu.make_async_remote_copy(
            src_ref=staged.at[other[1] * n_tm + other[0]],
            dst_ref=landed.at[tm + 1, own_boxes],
            send_sem=in_send,
            recv_sem=in_recv,
            device_id=other,
            device_id_type=MESH,
        ).start()

    lag = lax.broadcasted_iota(jnp.int32, (LANES, LANES), 1) - lax.broadcasted_iota(
        jnp.int32, (LANES, LANES), 0
    )
    causal = lag >= 0

    def split_rows(response):
        spread = jnp.broadcast_to(response, (LANES, LANES))
        turned = pltpu.roll(spread, 0, 1, stride=1, stride_axis=0)
        now = jnp.where(causal, turned, 0.0).astype(jnp.bfloat16)
        before = jnp.where(causal, 0.0, turned).astype(jnp.bfloat16)
        return before, now

    for fetch in fetches:
        fetch.wait()

    def build(offset, carry):
        responses = trans_rows[offset]
        column = pl.ds(pl.multiple_of(offset * LANES, LANES), LANES)
        for ray in range(SUBLANES):
            before, now = split_rows(responses[ray : ray + 1, :])
            trans_mats[ray, 0:LANES, column] = before
            trans_mats[ray, LANES : 2 * LANES, column] = now
        return carry

    lax.fori_loop(0, offsets, build, 0)
    for slot in range(slots):
        before, now = split_rows(near_rows[slot : slot + 1, :])
        near_mats[0:LANES, slot * LANES : (slot + 1) * LANES] = before
        near_mats[LANES : 2 * LANES, slot * LANES : (slot + 1) * LANES] = now
    wide[0:block_rows, :] = jnp.zeros((block_rows, LANES), jnp.float32)

    arrived = landed.at[pl.ds(1, n_tm)]
    pltpu.make_async_copy(arrived, arrived, in_recv).wait()

    for block in range(1, n_tm + 1):
        wide[block * block_rows : (block + 1) * block_rows, :] = (
            landed[block].astype(jnp.float32).reshape(block_rows, LANES)
        )

    far_rows = far_all.reshape(offsets, rows * SUBLANES, LANES)
    for ray in range(SUBLANES):
        blocks = wide[pl.ds(ray, rows + boxes, stride=SUBLANES), :].astype(jnp.bfloat16)
        pair = jnp.concatenate([blocks[:rows], blocks[boxes:]], axis=1)
        products = jnp.dot(pair, trans_mats[ray], preferred_element_type=jnp.float32)
        for offset in range(offsets):
            far_rows[offset, pl.ds(ray, rows, stride=SUBLANES), :] = products[
                :, offset * LANES : (offset + 1) * LANES
            ]

    for block in range(n_tm):
        low = block * block_rows
        pair = jnp.concatenate(
            [
                wide[low : low + block_rows, :].astype(jnp.bfloat16),
                wide[low + block_rows : low + 2 * block_rows, :].astype(jnp.bfloat16),
            ],
            axis=1,
        )
        products = jnp.dot(pair, near_mats[...], preferred_element_type=jnp.float32)
        for slot in range(slots):
            near_all[slot, block * boxes : (block + 1) * boxes] = products[
                :, slot * LANES : (slot + 1) * LANES
            ].reshape(boxes, SUBLANES, LANES)

    def selected(all_ref, table, count, box, block, by_slot):
        total = None
        for entry in range(count):
            origin = table[entry, box] if by_slot else table[box, entry]
            term = all_ref[entry, origin + block * boxes]
            total = term if total is None else total + term
        return total.astype(jnp.bfloat16).astype(jnp.float32)

    def finish(to_space):
        for nth in range(box_dev):
            box = to_space * box_dev + nth
            for block in range(n_tm):
                far = selected(far_all, sources, offsets, box, block, False)
                near = selected(near_all, nears, slots, box, block, True)
                leaving[block, box] = (far + near).astype(jnp.bfloat16)

    def dispatch(ds):
        to_space = wrapped(space + ds, n_space)
        to_boxes = pl.ds(to_space * box_dev, box_dev)
        for dt in range(n_tm):
            to_tm = wrapped(tm + dt, n_tm)
            if dt or ds:
                pltpu.make_async_remote_copy(
                    src_ref=leaving.at[to_tm, to_boxes],
                    dst_ref=out_ref.at[mine],
                    send_sem=out_send,
                    recv_sem=out_recv,
                    device_id=(to_tm, to_space),
                    device_id_type=MESH,
                ).start()
            else:
                pltpu.make_async_copy(
                    leaving.at[tm, to_boxes], out_ref.at[mine], out_recv
                ).start()

    order = sorted(range(n_space), key=lambda ds: -min(ds, n_space - ds))
    for nth, ds in enumerate(order):
        finish(wrapped(space + ds, n_space))
        if nth:
            dispatch(order[nth - 1])
    dispatch(order[-1])

    sent = staged.at[pl.ds(0, peers - 1)]
    pltpu.make_async_copy(sent, sent, in_send).wait()
    pltpu.make_async_copy(out_ref, out_ref, out_recv).wait()
    pltpu.make_async_copy(sent, sent, out_send).wait()


def fused_body(signal, source_boxes, near_boxes, trans_kernel, near_kernel):
    n_tm, n_space = lax.axis_size("tm"), lax.axis_size("space")
    peers = n_tm * n_space
    box_dev, rays, samples = signal.shape
    boxes = box_dev * n_space
    offsets, slots = trans_kernel.shape[0], near_kernel.shape[0]
    rows = n_tm * boxes
    grouped = signal.reshape(box_dev, peers, SUBLANES, samples)
    hbm = pl.BlockSpec(memory_space=pltpu.HBM)
    field = pl.pallas_call(
        functools.partial(fused_kernel, n_tm, n_space),
        out_shape=jax.ShapeDtypeStruct((peers, box_dev, SUBLANES, samples), jnp.bfloat16),
        in_specs=[hbm] * 5,
        out_specs=pl.BlockSpec(memory_space=pl.ANY),
        scratch_shapes=[
            pltpu.VMEM((peers, box_dev, SUBLANES, LANES), jnp.bfloat16),
            pltpu.VMEM((n_tm + 1, boxes, SUBLANES, LANES), jnp.bfloat16),
            pltpu.VMEM(((rows + boxes) * SUBLANES, LANES), jnp.float32),
            pltpu.VMEM((offsets, SUBLANES, LANES), jnp.float32),
            pltpu.VMEM((slots, LANES), jnp.float32),
            pltpu.VMEM((SUBLANES, 2 * LANES, offsets * LANES), jnp.bfloat16),
            pltpu.VMEM((2 * LANES, slots * LANES), jnp.bfloat16),
            pltpu.VMEM((offsets, rows, SUBLANES, LANES), jnp.float32),
            pltpu.VMEM((slots, rows, SUBLANES, LANES), jnp.float32),
            pltpu.VMEM((n_tm, boxes, SUBLANES, LANES), jnp.bfloat16),
            pltpu.SMEM(source_boxes.shape, jnp.int32),
            pltpu.SMEM(near_boxes.shape[::-1], jnp.int32),
            pltpu.SemaphoreType.DMA,
            pltpu.SemaphoreType.DMA,
            pltpu.SemaphoreType.DMA,
            pltpu.SemaphoreType.DMA,
            pltpu.SemaphoreType.DMA((4,)),
            pltpu.SemaphoreType.DMA((box_dev,)),
        ],
        compiler_params=pltpu.CompilerParams(
            collective_id=0, has_side_effects=True, vmem_limit_bytes=67043328
        ),
    )(grouped, source_boxes, near_boxes.T, trans_kernel, near_kernel)
    return field.transpose(1, 0, 2, 3).reshape(signal.shape)


def routed(signal, source_boxes, near_boxes, trans_kernel, near_kernel):
    n_tm, n_space = lax.axis_size("tm"), lax.axis_size("space")
    box_dev, rays, samples = signal.shape
    rows = n_tm * n_space * box_dev
    fits = rays == n_tm * n_space * SUBLANES and samples == LANES and rows <= 2 * LANES
    chosen = fused_body if fits else body
    return chosen(signal, source_boxes, near_boxes, trans_kernel, near_kernel)


def solution(mesh):
    in_specs = (P("space", None, "tm"), P(), P(), P(None, "space", None), P())
    out_specs = P("space", None, "tm")
    return jax.shard_map(
        routed, mesh=mesh, in_specs=in_specs, out_specs=out_specs, check_vma=False
    )
```

```python
import functools

import jax
import jax.numpy as jnp
from jax import lax
from jax.experimental import pallas as pl
from jax.experimental.pallas import tpu as pltpu
from jax.sharding import PartitionSpec as P

REACH = 2
MESH = pl.DeviceIdType.MESH
LANES = 128
SUBLANES = 8
def from_behind(shard, axis, by):
    size = lax.axis_size(axis)
    pairs = [(i, i + by) for i in range(size) if 0 <= i + by < size]
    return lax.ppermute(shard, axis, pairs)


def with_halo(block, sides, width):
    for axis, dim in sides:
        count = lax.axis_size(axis)
        forward = [(i, i + 1) for i in range(count - 1)]
        backward = [(target, source) for source, target in forward]
        low = lax.ppermute(
            lax.slice_in_dim(block, block.shape[dim] - width, None, axis=dim), axis, forward
        )
        high = lax.ppermute(lax.slice_in_dim(block, 0, width, axis=dim), axis, backward)
        block = jnp.concatenate([low, block, high], axis=dim)
    return block


def block_matrix(kernel):
    blocklen = kernel.shape[-1]
    leading = kernel.shape[:-1]
    zeroes = jnp.zeros(leading + (2 * blocklen,), jnp.bfloat16)
    widened = jnp.concatenate([zeroes, kernel.astype(jnp.bfloat16)], axis=-1)
    tiled = jnp.tile(widened, (1,) * len(leading) + (2 * blocklen,))
    trimmed = tiled[..., : 2 * blocklen * (3 * blocklen - 1)]
    skewed = trimmed.reshape(leading + (2 * blocklen, 3 * blocklen - 1))
    return skewed[..., :blocklen]


def body(signal, source_boxes, near_boxes, trans_kernel, near_kernel):
    box_dev = signal.shape[0]
    current_rays = lax.all_to_all(signal, "space", split_axis=1, concat_axis=0, tiled=True)
    earlier_rays = from_behind(current_rays, "tm", 1)
    pair_rays = jnp.concatenate([earlier_rays, current_rays], axis=-1)
    offsets = source_boxes.shape[1]
    far = jnp.zeros(current_rays.shape, jnp.float32)
    for offset in range(offsets):
        trans_mats = block_matrix(trans_kernel[offset])
        rows = jnp.take(pair_rays, source_boxes[:, offset], axis=0)
        far = far + jnp.einsum("brs,rst->brt", rows, trans_mats, preferred_element_type=jnp.float32)
    far_rays = far.astype(jnp.bfloat16)
    near_mats = block_matrix(near_kernel)
    slots = near_boxes.shape[1]
    earlier_box = from_behind(signal, "tm", 1)
    pair_box = jnp.concatenate([earlier_box, signal], axis=-1)
    padded = with_halo(pair_box, (("space", 0),), REACH)
    first = lax.axis_index("space") * box_dev
    own_near = lax.dynamic_slice_in_dim(near_boxes, first, box_dev, 0)
    local_rows = own_near - (first - REACH)
    near_sum = jnp.zeros(signal.shape, jnp.float32)
    for slot in range(slots):
        rows = jnp.take(padded, local_rows[:, slot], axis=0)
        near_sum = near_sum + jnp.einsum(
            "brs,st->brt", rows, near_mats[slot], preferred_element_type=jnp.float32
        )
    near_box = near_sum.astype(jnp.bfloat16)
    far_box = lax.all_to_all(far_rays, "space", split_axis=0, concat_axis=1, tiled=True)
    return (far_box.astype(jnp.float32) + near_box.astype(jnp.float32)).astype(jnp.bfloat16)


def fused_kernel(
    n_tm,
    n_space,
    signal_ref,
    source_ref,
    near_ref,
    trans_ref,
    kernel_ref,
    out_ref,
    staged,
    landed,
    wide,
    flat,
    trans_rows,
    near_rows,
    trans_mats,
    near_mats,
    far_all,
    near_all,
    leaving,
    sources,
    nears,
    in_send,
    in_recv,
    out_send,
    out_recv,
    local_sem,
    stage_sem,
):
    tm, space = lax.axis_index("tm"), lax.axis_index("space")
    peers = n_tm * n_space
    box_dev = signal_ref.shape[0]
    boxes = n_space * box_dev
    offsets = trans_ref.shape[0]
    slots = kernel_ref.shape[0]
    rows = n_tm * boxes
    block_rows = boxes * SUBLANES

    def wrapped(value, size):
        return jnp.where(value >= size, value - size, value)

    order = sorted(range(n_space), key=lambda ds: -min(ds, n_space - ds))
    others = [
        (wrapped(tm + dt, n_tm), wrapped(space + ds, n_space))
        for ds in order
        for dt in reversed(range(n_tm))
        if dt or ds
    ]
    mine = space * n_tm + tm
    own_boxes = pl.ds(space * box_dev, box_dev)

    first_ray = pl.multiple_of(tm * SUBLANES, SUBLANES)
    fetches = [
        pltpu.make_async_copy(
            trans_ref.at[:, pl.ds(first_ray, SUBLANES), :], trans_rows, local_sem.at[0]
        ),
        pltpu.make_async_copy(kernel_ref, near_rows, local_sem.at[1]),
        pltpu.make_async_copy(source_ref, sources, local_sem.at[2]),
        pltpu.make_async_copy(near_ref, nears, local_sem.at[3]),
    ]
    stagings = [
        pltpu.make_async_copy(signal_ref.at[nth], staged.at[:, nth], stage_sem.at[nth])
        for nth in range(box_dev)
    ]
    for fetch in stagings:
        fetch.start()
    barrier = pltpu.get_barrier_semaphore()
    for other in others:
        pl.semaphore_signal(barrier, inc=1, device_id=other, device_id_type=MESH)
    for fetch in fetches:
        fetch.start()
    pltpu.make_async_copy(signal_ref.at[:, mine], landed.at[tm + 1, own_boxes], in_recv).start()
    for staging in stagings:
        staging.wait()
    pl.semaphore_wait(barrier, peers - 1)
    for other in others:
        pltpu.make_async_remote_copy(
            src_ref=staged.at[other[1] * n_tm + other[0]],
            dst_ref=landed.at[tm + 1, own_boxes],
            send_sem=in_send,
            recv_sem=in_recv,
            device_id=other,
            device_id_type=MESH,
        ).start()

    lag = lax.broadcasted_iota(jnp.int32, (LANES, LANES), 1) - lax.broadcasted_iota(
        jnp.int32, (LANES, LANES), 0
    )
    causal = lag >= 0

    def split_rows(response):
        spread = jnp.broadcast_to(response, (LANES, LANES))
        turned = pltpu.roll(spread, 0, 1, stride=1, stride_axis=0)
        now = jnp.where(causal, turned, 0.0).astype(jnp.bfloat16)
        before = jnp.where(causal, 0.0, turned).astype(jnp.bfloat16)
        return before, now

    for fetch in fetches:
        fetch.wait()

    def build(offset, carry):
        responses = trans_rows[offset]
        column = pl.ds(pl.multiple_of(offset * LANES, LANES), LANES)
        for ray in range(SUBLANES):
            before, now = split_rows(responses[ray : ray + 1, :])
            trans_mats[ray, 0:LANES, column] = before
            trans_mats[ray, LANES : 2 * LANES, column] = now
        return carry

    lax.fori_loop(0, offsets, build, 0)
    for slot in range(slots):
        before, now = split_rows(near_rows[slot : slot + 1, :])
        near_mats[0:LANES, slot * LANES : (slot + 1) * LANES] = before
        near_mats[LANES : 2 * LANES, slot * LANES : (slot + 1) * LANES] = now
    wide[0:block_rows, :] = jnp.zeros((block_rows, LANES), jnp.float32)
    flat[0:block_rows, :] = jnp.zeros((block_rows, LANES), jnp.bfloat16)

    arrived = landed.at[pl.ds(1, n_tm)]
    pltpu.make_async_copy(arrived, arrived, in_recv).wait()

    for block in range(1, n_tm + 1):
        these = landed[block].astype(jnp.float32).reshape(block_rows, LANES)
        wide[block * block_rows : (block + 1) * block_rows, :] = these
        flat[block * block_rows : (block + 1) * block_rows, :] = these.astype(jnp.bfloat16)

    far_rows = far_all.reshape(offsets, rows * SUBLANES, LANES)
    for ray in range(SUBLANES):
        blocks = wide[pl.ds(ray, rows + boxes, stride=SUBLANES), :].astype(jnp.bfloat16)
        pair = jnp.concatenate([blocks[:rows], blocks[boxes:]], axis=1)
        products = jnp.dot(pair, trans_mats[ray], preferred_element_type=jnp.float32)
        for offset in range(offsets):
            far_rows[offset, pl.ds(ray, rows, stride=SUBLANES), :] = products[
                :, offset * LANES : (offset + 1) * LANES
            ]

    for tile in range(0, slots, 2):
        taken = min(2, slots - tile)
        products = jnp.dot(
            jnp.concatenate(
                [flat[0 : n_tm * block_rows, :], flat[block_rows:, :]], axis=1
            ),
            near_mats[:, tile * LANES : (tile + taken) * LANES],
            preferred_element_type=jnp.float32,
        )
        for nth in range(taken):
            near_all[tile + nth] = products[:, nth * LANES : (nth + 1) * LANES].reshape(
                rows, SUBLANES, LANES
            )

    def selected(all_ref, table, count, box, block, by_slot):
        total = None
        for entry in range(count):
            origin = table[entry, box] if by_slot else table[box, entry]
            term = all_ref[entry, origin + block * boxes]
            total = term if total is None else total + term
        return total.astype(jnp.bfloat16).astype(jnp.float32)

    def finish(to_space):
        for nth in range(box_dev):
            box = to_space * box_dev + nth
            for block in range(n_tm):
                far = selected(far_all, sources, offsets, box, block, False)
                near = selected(near_all, nears, slots, box, block, True)
                leaving[block, box] = (far + near).astype(jnp.bfloat16)

    def dispatch(ds):
        to_space = wrapped(space + ds, n_space)
        to_boxes = pl.ds(to_space * box_dev, box_dev)
        for dt in range(n_tm):
            to_tm = wrapped(tm + dt, n_tm)
            if dt or ds:
                pltpu.make_async_remote_copy(
                    src_ref=leaving.at[to_tm, to_boxes],
                    dst_ref=out_ref.at[:, mine],
                    send_sem=out_send,
                    recv_sem=out_recv,
                    device_id=(to_tm, to_space),
                    device_id_type=MESH,
                ).start()
            else:
                pltpu.make_async_copy(
                    leaving.at[tm, to_boxes], out_ref.at[:, mine], out_recv
                ).start()

    for nth, ds in enumerate(order):
        finish(wrapped(space + ds, n_space))
        if nth:
            dispatch(order[nth - 1])
    dispatch(order[-1])

    sent = staged.at[pl.ds(0, peers - 1)]
    pltpu.make_async_copy(sent, sent, in_send).wait()
    pltpu.make_async_copy(out_ref, out_ref, out_recv).wait()
    pltpu.make_async_copy(sent, sent, out_send).wait()


def fused_body(signal, source_boxes, near_boxes, trans_kernel, near_kernel):
    n_tm, n_space = lax.axis_size("tm"), lax.axis_size("space")
    peers = n_tm * n_space
    box_dev, rays, samples = signal.shape
    boxes = box_dev * n_space
    offsets, slots = trans_kernel.shape[0], near_kernel.shape[0]
    rows = n_tm * boxes
    grouped = signal.reshape(box_dev, peers, SUBLANES, samples)
    hbm = pl.BlockSpec(memory_space=pltpu.HBM)
    field = pl.pallas_call(
        functools.partial(fused_kernel, n_tm, n_space),
        out_shape=pltpu.VMEM(grouped.shape, jnp.bfloat16),
        in_specs=[hbm] * 5,
        out_specs=pl.BlockSpec(memory_space=pl.ANY),
        scratch_shapes=[
            pltpu.VMEM((peers, box_dev, SUBLANES, LANES), jnp.bfloat16),
            pltpu.VMEM((n_tm + 1, boxes, SUBLANES, LANES), jnp.bfloat16),
            pltpu.VMEM(((rows + boxes) * SUBLANES, LANES), jnp.float32),
            pltpu.VMEM(((rows + boxes) * SUBLANES, LANES), jnp.bfloat16),
            pltpu.VMEM((offsets, SUBLANES, LANES), jnp.float32),
            pltpu.VMEM((slots, LANES), jnp.float32),
            pltpu.VMEM((SUBLANES, 2 * LANES, offsets * LANES), jnp.bfloat16),
            pltpu.VMEM((2 * LANES, slots * LANES), jnp.bfloat16),
            pltpu.VMEM((offsets, rows, SUBLANES, LANES), jnp.float32),
            pltpu.VMEM((slots, rows, SUBLANES, LANES), jnp.float32),
            pltpu.VMEM((n_tm, boxes, SUBLANES, LANES), jnp.bfloat16),
            pltpu.SMEM(source_boxes.shape, jnp.int32),
            pltpu.SMEM(near_boxes.shape[::-1], jnp.int32),
            pltpu.SemaphoreType.DMA,
            pltpu.SemaphoreType.DMA,
            pltpu.SemaphoreType.DMA,
            pltpu.SemaphoreType.DMA,
            pltpu.SemaphoreType.DMA((4,)),
            pltpu.SemaphoreType.DMA((box_dev,)),
        ],
        compiler_params=pltpu.CompilerParams(
            collective_id=0, has_side_effects=True, vmem_limit_bytes=60*1024*1024
        ),
    )(*[pltpu.with_memory_space_constraint(x, pltpu.HBM) for x in (grouped, source_boxes, near_boxes.T, trans_kernel, near_kernel)])
    return field.reshape(signal.shape)


def routed(signal, source_boxes, near_boxes, trans_kernel, near_kernel):
    n_tm, n_space = lax.axis_size("tm"), lax.axis_size("space")
    box_dev, rays, samples = signal.shape
    rows = n_tm * n_space * box_dev
    fits = rays == n_tm * n_space * SUBLANES and samples == LANES and rows <= 2 * LANES
    chosen = fused_body if fits else body
    return chosen(signal, source_boxes, near_boxes, trans_kernel, near_kernel)


def solution(mesh):
    in_specs = (P("space", None, "tm"), P(), P(), P(None, "space", None), P())
    out_specs = P("space", None, "tm")
    return jax.shard_map(
        routed, mesh=mesh, in_specs=in_specs, out_specs=out_specs, check_vma=False
    )
```
